32 devices in a mesh: row: 2 (over y), col: 16 (over z, x, core).
Axes of the slice: x: 2, y: 2, z: 4, core: 2. Of those that a mesh axis runs over, the one named last changes fastest.
Arguments:
- blocks: bfloat16 [128, 2048, 128], P('row', 'col'), may hold values from -0.1875 to 0.1875
- block_rows: int32 [2, 1024], P('row', 'col'), may hold values from 0 to 2047, as said below
- block_cols: int32 [2, 1024], P('row', 'col'), may hold values from 0 to 255
- counts: int32 [2, 16], P('row', 'col'), may hold values from 1 to 64, as said below
- start_vectors: float32 [32, 524288], P(None, ('row', 'col')), may hold values from -6 to 6
Outputs:
- vectors: float32 [32, 524288], P(None, ('row', 'col'))
The draws below stay inside these ranges and needn't reach their ends.
Inputs may be any that keep to these rules, and one draw needn't show every extreme that they name: counts[r, c] is the number of live slots of grid position (r, c); in every draw some position has all 64 slots live. For every grid position (r, c) and every o < 16, exactly 4 of its 64 slots have block_rows[r, c * 64 + s] // 128 == o.
All inputs are finite; a program needn't handle non-finite values.
Results may differ from the reference program's by a relative error of at most 0.0036.
Values may be sent and summed in bfloat16 or wider, within the bound.
A program may use at most 256 MiB of HBM per device.

```python
import jax
import jax.numpy as jnp
from jax import lax

N = 524288
K = 32
BS = 128
SLOTS = 64
ITERS = 2
PB = 128
CB = 256
N_ROW = 2
N_COL = 16


def draw_counts(key, part):
    first_key = jax.random.fold_in(key, 11)
    second_key = jax.random.fold_in(key, 23)
    uniform_ints = jax.random.randint(first_key, (N_ROW * N_COL,), 1, SLOTS + 1)
    skewed = jnp.clip(uniform_ints * uniform_ints // SLOTS, 1, SLOTS)
    fullest = jax.random.randint(second_key, (), 0, N_ROW * N_COL)
    skewed = jnp.where(jnp.arange(N_ROW * N_COL) == fullest, SLOTS, skewed)
    return skewed.reshape(N_ROW, N_COL).astype(jnp.int32)


def draw_block_rows(key, part):
    order_key = jax.random.fold_in(key, 5)
    offset_key = jax.random.fold_in(key, 7)
    tile_total = N_ROW * N_COL
    owner_base = jnp.tile(jnp.arange(N_COL, dtype=jnp.int32), SLOTS // N_COL)
    tile_keys = jax.random.split(order_key, tile_total)
    owners = jax.vmap(lambda one_key: jax.random.permutation(one_key, owner_base))(tile_keys)
    offsets = jax.random.randint(offset_key, (tile_total, SLOTS), 0, PB)
    return (owners * PB + offsets).reshape(N_ROW, N_COL * SLOTS).astype(jnp.int32)


def set_ends(values, rng, smallest, high):
    place = [jax.random.randint(jax.random.fold_in(rng, axis), (), 0, length) for axis, length in enumerate(values.shape)]
    widest = values.shape.index(max(values.shape))
    next_to = place[:widest] + [(place[widest] + 1) % values.shape[widest]] + place[widest + 1:]
    return values.at[tuple(place)].set(smallest).at[tuple(next_to)].set(high)


def block_scale(own_key, extent, cuts, least, largest):
    factor_of = 1.0
    for axis_at, blocks in cuts:
        heights = jax.random.uniform(jax.random.fold_in(jax.random.fold_in(own_key, 6), axis_at), (blocks,), jnp.float32, least / len(cuts), largest / len(cuts))
        factor_of = factor_of * jnp.repeat(jnp.exp(heights), extent[axis_at] // blocks).reshape((-1,) + (1,) * (len(extent) - 1 - axis_at))
    return factor_of


def bell_draw(stream_key, dims, scale, bound, cuts=(), kind=jnp.bfloat16):
    result = scale * jax.random.normal(stream_key, dims, jnp.float32)
    if cuts:
        result = result * block_scale(stream_key, dims, cuts, -0.22, 0.18)
    return jnp.clip(result, -bound, bound).astype(kind)


def setup_inputs(seed: int = 0) -> dict:
    seeds = jax.random.split(jax.random.key(seed), 6)
    return {
        "blocks": bell_draw(seeds[0], (N_ROW * SLOTS, N_COL * BS, BS), (BS * 8) ** -0.5, 0.1875, ((0, 2), (1, 16))),
        "block_rows": draw_block_rows(jax.random.fold_in(seeds[5], 71), 0),
        "block_cols": set_ends(jax.random.randint(seeds[2], (N_ROW, N_COL * SLOTS), 0, CB), jax.random.fold_in(seeds[2], 1), 0, CB - 1).astype(jnp.int32),
        "counts": draw_counts(jax.random.fold_in(seeds[5], 71), 0),
        "start_vectors": bell_draw(seeds[4], (K, N), 1.0, 6.0, ((1, 32),), jnp.float32),
    }


def cholesky_lower(gram_matrix):
    matrix_order = gram_matrix.shape[0]
    positions = jnp.arange(matrix_order)

    def column_step(position, factor):
        before = (positions < position).astype(gram_matrix.dtype)
        target_row = lax.dynamic_index_in_dim(factor, position, 0, keepdims=False) * before
        column = lax.dynamic_index_in_dim(gram_matrix, position, 1, keepdims=False)
        residue = column - lax.optimization_barrier(jnp.sum(factor * target_row[None, :], axis=1))
        on_diagonal = positions == position
        pivot_value = jnp.sqrt(jnp.sum(jnp.where(on_diagonal, residue, 0.0)))
        values = jnp.where(on_diagonal, pivot_value, residue / pivot_value)
        values = jnp.where(positions >= position, values, 0.0)
        return lax.dynamic_update_index_in_dim(factor, values, position, 1)
    return lax.fori_loop(0, matrix_order, column_step, jnp.zeros_like(gram_matrix))

def lower_inverse(lower_factor):
    matrix_order = lower_factor.shape[0]
    positions = jnp.arange(matrix_order)

    def row_step(position, inverse):
        lower_row = lax.dynamic_index_in_dim(lower_factor, position, 0, keepdims=False)
        before = (positions < position).astype(lower_factor.dtype)
        inner_sum = lax.optimization_barrier(jnp.sum((lower_row * before)[:, None] * inverse, axis=0))
        unit_row = (positions == position).astype(lower_factor.dtype)
        pivot_value = jnp.sum(lower_row * unit_row)
        return lax.dynamic_update_index_in_dim(inverse, (unit_row - inner_sum) / pivot_value, position, 0)
    return lax.fori_loop(0, matrix_order, row_step, jnp.zeros_like(lower_factor))

def reference(blocks, block_rows, block_cols, counts, start_vectors):
    block_count = N // BS
    row_span = PB * N_COL
    slot_ids = jnp.arange(SLOTS, dtype=jnp.int32)
    tile_order = jnp.arange(N_ROW * N_COL, dtype=jnp.int32)
    vectors = start_vectors
    for iteration in range(ITERS):
        narrow = lax.optimization_barrier(vectors.astype(jnp.bfloat16))
        rounded = narrow.astype(jnp.float32).reshape(K, block_count, BS)

        def one_tile(image_rows, tile_index):
            grid_row = tile_index // N_COL
            grid_col = tile_index % N_COL
            tile_blocks = lax.dynamic_slice(blocks, (grid_row * SLOTS, grid_col * BS, jnp.int32(0)), (SLOTS, BS, BS)).astype(jnp.float32)
            local_rows = lax.dynamic_slice(block_rows, (grid_row, grid_col * SLOTS), (1, SLOTS))[0].astype(jnp.int32)
            local_cols = lax.dynamic_slice(block_cols, (grid_row, grid_col * SLOTS), (1, SLOTS))[0].astype(jnp.int32)
            live_count = lax.dynamic_slice(counts, (grid_row, grid_col), (1, 1))[0, 0]
            global_rows = grid_row * row_span + local_rows
            global_cols = local_cols // PB * row_span + grid_col * PB + local_cols % PB
            live_mask = (slot_ids < live_count).astype(jnp.float32)
            from_cols = jnp.take(rounded, global_cols, axis=1)
            from_rows = jnp.take(rounded, global_rows, axis=1)
            to_rows = jnp.einsum('kgj,gij->kgi', from_cols, tile_blocks, precision=lax.Precision.HIGHEST) * live_mask[None, :, None]
            to_cols = jnp.einsum('kgi,gij->kgj', from_rows, tile_blocks, precision=lax.Precision.HIGHEST) * live_mask[None, :, None]
            image_rows = image_rows.at[:, global_rows].add(to_rows)
            image_rows = image_rows.at[:, global_cols].add(to_cols)
            return (image_rows, None)
        image_rows = lax.scan(one_tile, jnp.zeros((K, block_count, BS), jnp.float32), tile_order)[0]
        product = image_rows.reshape(K, N)
        gram_matrix = jnp.dot(product, product.T, precision=lax.Precision.HIGHEST, preferred_element_type=jnp.float32) / N
        inverse = lower_inverse(cholesky_lower(gram_matrix))
        vectors = jnp.dot(inverse, product, precision=lax.Precision.HIGHEST, preferred_element_type=jnp.float32)
    return vectors
```

```python
import functools

import jax
import jax.numpy as jnp
from jax import lax
from jax.experimental import pallas as pl
from jax.experimental.pallas import tpu as pltpu
from jax.sharding import PartitionSpec as P

ITERS = 2
MESH = pl.DeviceIdType.MESH
ANY = pl.BlockSpec(memory_space=pl.ANY)
VMEM = pl.BlockSpec(memory_space=pltpu.VMEM)
SMEM = pl.BlockSpec(memory_space=pltpu.SMEM)
VMEM_BYTES = 48 << 20


def greet(n_row, n_col):
    my_row, my_col = lax.axis_index("row"), lax.axis_index("col")
    barrier = pltpu.get_barrier_semaphore()
    for d in range(1, n_col):
        peer = lax.rem(my_col + d, n_col)
        pl.semaphore_signal(barrier, inc=1, device_id=(my_row, peer), device_id_type=MESH)
    for d in range(1, n_row):
        peer = lax.rem(my_row + d, n_row)
        pl.semaphore_signal(barrier, inc=1, device_id=(peer, my_col), device_id_type=MESH)
    pl.semaphore_wait(barrier, n_col + n_row - 2)
    return my_row, my_col


def exchange_kernel(n_row, n_col, c_src, r_src, c_dst, r_dst, own, c_send, c_recv, r_send, r_recv):
    my_row, my_col = greet(n_row, n_col)
    shared = r_src.shape[0] == 1
    copies = []
    for d in range(1, n_row):
        peer = lax.rem(my_row + d, n_row)
        copies.append(
            pltpu.make_async_remote_copy(
                src_ref=r_src.at[0 if shared else peer],
                dst_ref=r_dst.at[my_row],
                send_sem=r_send.at[d],
                recv_sem=r_recv.at[d],
                device_id=(peer, my_col),
                device_id_type=MESH,
            )
        )
    for d in range(1, n_col):
        peer = lax.rem(my_col + d, n_col)
        copies.append(
            pltpu.make_async_remote_copy(
                src_ref=c_src.at[peer],
                dst_ref=c_dst.at[my_col],
                send_sem=c_send.at[d],
                recv_sem=c_recv.at[d],
                device_id=(my_row, peer),
                device_id_type=MESH,
            )
        )
    copies.append(pltpu.make_async_copy(c_src.at[my_col], c_dst.at[my_col], own.at[0]))
    copies.append(
        pltpu.make_async_copy(r_src.at[0 if shared else my_row], r_dst.at[my_row], own.at[1])
    )
    for copy in copies:
        copy.start()
    for copy in copies:
        copy.wait()


def exchange(n_row, n_col, collective_id, c_src, r_src):
    return pl.pallas_call(
        functools.partial(exchange_kernel, n_row, n_col),
        out_shape=(
            jax.ShapeDtypeStruct(c_src.shape, c_src.dtype),
            jax.ShapeDtypeStruct((n_row,) + r_src.shape[1:], r_src.dtype),
        ),
        in_specs=[ANY, ANY],
        out_specs=(ANY, ANY),
        scratch_shapes=[
            pltpu.SemaphoreType.DMA((2,)),
            pltpu.SemaphoreType.DMA((n_col,)),
            pltpu.SemaphoreType.DMA((n_col,)),
            pltpu.SemaphoreType.DMA((n_row,)),
            pltpu.SemaphoreType.DMA((n_row,)),
        ],
        compiler_params=pltpu.CompilerParams(collective_id=collective_id, has_side_effects=True),
    )(c_src, r_src)


def split(value):
    high = value.astype(jnp.bfloat16)
    return high, (value - high.astype(jnp.float32)).astype(jnp.bfloat16)


def inverse_stack(inverse):
    high, low = split(inverse)
    return jnp.concatenate([high, low, high, low], axis=1)


def apply_inverse(stacked, product):
    high, low = split(product)
    parts = jnp.concatenate([high, high, low, low], axis=0)
    return jnp.dot(stacked, parts, preferred_element_type=jnp.float32)


def pack_kernel(first, wanted, all_cols, source, *rest):
    if first:
        c_out, r_out, held = rest
        for b in range(held.shape[0]):
            held[b] = source[:, b * 128 : (b + 1) * 128].astype(jnp.bfloat16)
    else:
        inverse, c_out, r_out, held = rest
        stacked = inverse_stack(inverse[...])

        def round_block(b, carry):
            held[b] = apply_inverse(stacked, source[b]).astype(jnp.bfloat16)
            return carry

        lax.fori_loop(0, held.shape[0], round_block, 0, unroll=8)
    panel = held.shape[0]
    base = lax.axis_index("row") * panel

    def one_c(t, carry):
        c_out[t] = held[wanted[t]]
        return carry

    lax.fori_loop(0, c_out.shape[0], one_c, 0, unroll=8)
    for p in range(all_cols.shape[0]):

        def one_r(t, carry):
            r_out[p, t] = held[jnp.clip(all_cols[p, t] - base, 0, panel - 1)]
            return carry

        lax.fori_loop(0, r_out.shape[1], one_r, 0, unroll=8)


def multiply_kernel(panel, perm, cols, live, blocks, from_rows, from_cols, to_rows, to_cols):
    def one_slot(t, carry):
        block = blocks[perm[t]]
        alive = live[t] > 0
        x_row = from_rows[t]
        x_col = from_cols[cols[t] // panel, t]
        row_product = lax.dot_general(
            x_col, block, (((1,), (1,)), ((), ())), preferred_element_type=jnp.float32
        )
        col_product = jnp.dot(x_row, block, preferred_element_type=jnp.float32)
        to_rows[t] = jnp.where(alive, row_product, 0.0).astype(jnp.bfloat16)
        to_cols[t] = jnp.where(alive, col_product, 0.0).astype(jnp.bfloat16)
        return carry

    lax.fori_loop(0, blocks.shape[0], one_slot, 0, unroll=8)


def sum_kernel(wanted, all_cols, row_terms, col_terms, product, gram):
    panel, vectors = product.shape[0], product.shape[1]
    base = lax.axis_index("row") * panel
    product[...] = jnp.zeros_like(product)

    def one_row(t, carry):
        at = wanted[t]
        product[at] = product[at] + row_terms[t].astype(jnp.float32)
        return carry

    lax.fori_loop(0, row_terms.shape[0], one_row, 0, unroll=4)
    for p in range(all_cols.shape[0]):

        def one_col(t, carry):
            at = all_cols[p, t] - base

            @pl.when((at >= 0) & (at < panel))
            def _():
                product[at] = product[at] + col_terms[p, t].astype(jnp.float32)

            return carry

        lax.fori_loop(0, col_terms.shape[1], one_col, 0, unroll=4)

    def one_gram(b, total):
        high, low = split(product[b])
        parts = jnp.concatenate([high, low], axis=0)
        return total + lax.dot_general(
            parts, parts, (((1,), (1,)), ((), ())), preferred_element_type=jnp.float32
        )

    total = lax.fori_loop(
        0, panel, one_gram, jnp.zeros((2 * vectors, 2 * vectors), jnp.float32), unroll=8
    )
    upper = total[:vectors] + total[vectors:]
    full = upper[:, :vectors] + upper[:, vectors:]
    gram[...] = jnp.concatenate([full[8 * i : 8 * i + 8] for i in range(vectors // 8)], axis=1)


def factor_kernel(
    n_row, n_col, order, gram, inverse, row_in, row_sum, col_in, r_send, r_recv, c_send, c_recv
):
    my_row, my_col = greet(n_row, n_col)
    copies = []
    for d in range(1, n_row):
        peer = lax.rem(my_row + d, n_row)
        copies.append(
            pltpu.make_async_remote_copy(
                src_ref=gram,
                dst_ref=row_in.at[my_row],
                send_sem=r_send.at[d],
                recv_sem=r_recv.at[d],
                device_id=(peer, my_col),
                device_id_type=MESH,
            )
        )
    for copy in copies:
        copy.start()
    row_in[my_row] = gram[...]
    for copy in copies:
        copy.wait()
    row_sum[...] = jnp.sum(row_in[...], axis=0)
    copies = []
    for d in range(1, n_col):
        peer = lax.rem(my_col + d, n_col)
        copies.append(
            pltpu.make_async_remote_copy(
                src_ref=row_sum,
                dst_ref=col_in.at[my_col],
                send_sem=c_send.at[d],
                recv_sem=c_recv.at[d],
                device_id=(my_row, peer),
                device_id_type=MESH,
            )
        )
    for copy in copies:
        copy.start()
    col_in[my_col] = row_sum[...]
    for copy in copies:
        copy.wait()
    packed = jnp.sum(col_in[...], axis=0) / order
    size = inverse.shape[0]
    full = jnp.concatenate([packed[:, size * i : size * (i + 1)] for i in range(size // 8)], axis=0)
    rows = lax.broadcasted_iota(jnp.int32, (size, size), 0)
    lanes = lax.broadcasted_iota(jnp.int32, (size, size), 1)
    work = jnp.concatenate([full, (rows == lanes).astype(jnp.float32)], axis=1)
    row_ids = lax.broadcasted_iota(jnp.int32, (size, 2 * size), 0)
    for j in range(size):
        scale = 1.0 / jnp.sqrt(work[j : j + 1, j : j + 1])
        pivot_row = work[j : j + 1, :] * scale
        factors = work[:, j : j + 1] * scale
        work = jnp.where(
            row_ids > j, work - factors * pivot_row, jnp.where(row_ids == j, pivot_row, work)
        )
    inverse[...] = work[:, size:]


def finish_kernel(source, inverse, out):
    stacked = inverse_stack(inverse[...])
    for b in range(source.shape[0]):
        out[:, b * 128 : (b + 1) * 128] = apply_inverse(stacked, source[b])


def local_params():
    return pltpu.CompilerParams(vmem_limit_bytes=VMEM_BYTES)


def per_device(n_row, n_col, blocks, block_rows, block_cols, counts, start_vectors):
    slots, size = blocks.shape[0], blocks.shape[1]
    vectors, width = start_vectors.shape
    panel = width // size
    share = slots // n_col
    bf16, f32 = jnp.bfloat16, jnp.float32
    shape = jax.ShapeDtypeStruct

    rows, cols, ids = block_rows[0], block_cols[0], jnp.arange(slots, dtype=jnp.int32)
    owner = rows // panel
    earlier = (owner[None, :] == owner[:, None]) & (ids[None, :] < ids[:, None])
    place = owner * share + jnp.sum(earlier.astype(jnp.int32), axis=1)
    here = (place[None, :] == ids[:, None]).astype(jnp.int32)
    perm = jnp.sum(here * ids[None, :], axis=1)
    rows = jnp.sum(here * rows[None, :], axis=1)
    cols = jnp.sum(here * cols[None, :], axis=1)
    live = (perm < counts[0, 0]).astype(jnp.int32)

    row_ask = jnp.pad((rows % panel).reshape(n_col, 1, share), ((0, 0), (0, 7), (0, 128 - share)))
    col_ask = jnp.pad(cols.reshape(1, 1, slots), ((0, 0), (0, 7), (0, 128 - slots)))
    row_got, col_got = exchange(n_row, n_col, 0, row_ask, col_ask)
    wanted = row_got[:, 0, :share].reshape(slots)
    all_cols = col_got[:, 0, :slots]

    product = inverse = None
    for iteration in range(ITERS):
        first = iteration == 0
        sources = (start_vectors,) if first else (product, inverse)
        c_src, r_src = pl.pallas_call(
            functools.partial(pack_kernel, first),
            out_shape=(
                shape((slots, vectors, size), bf16),
                shape((n_row, slots, vectors, size), bf16),
            ),
            in_specs=[SMEM, SMEM] + [VMEM] * len(sources),
            out_specs=(VMEM, VMEM),
            scratch_shapes=[pltpu.VMEM((panel, vectors, size), bf16)],
            compiler_params=local_params(),
        )(wanted, all_cols, *sources)
        from_rows, from_cols = exchange(
            n_row, n_col, 1, c_src.reshape(n_col, share, vectors, size), r_src
        )
        to_rows, to_cols = pl.pallas_call(
            functools.partial(multiply_kernel, panel),
            out_shape=(shape((slots, vectors, size), bf16),) * 2,
            in_specs=[SMEM] * 3 + [VMEM] * 3,
            out_specs=(VMEM, VMEM),
            compiler_params=local_params(),
        )(perm, cols, live, blocks, from_rows.reshape(slots, vectors, size), from_cols)
        row_terms, col_terms = exchange(
            n_row, n_col, 2, to_rows.reshape(n_col, share, vectors, size), to_cols[None]
        )
        product, gram = pl.pallas_call(
            sum_kernel,
            out_shape=(shape((panel, vectors, size), f32), shape((8, vectors * vectors // 8), f32)),
            in_specs=[SMEM, SMEM, VMEM, VMEM],
            out_specs=(VMEM, VMEM),
            compiler_params=local_params(),
        )(wanted, all_cols, row_terms.reshape(slots, vectors, size), col_terms)
        packed = pltpu.VMEM(gram.shape, f32)
        inverse = pl.pallas_call(
            functools.partial(factor_kernel, n_row, n_col, float(n_row * n_col * width)),
            out_shape=shape((vectors, vectors), f32),
            in_specs=[VMEM],
            out_specs=VMEM,
            scratch_shapes=[
                pltpu.VMEM((n_row,) + gram.shape, f32),
                packed,
                pltpu.VMEM((n_col,) + gram.shape, f32),
                pltpu.SemaphoreType.DMA((n_row,)),
                pltpu.SemaphoreType.DMA((n_row,)),
                pltpu.SemaphoreType.DMA((n_col,)),
                pltpu.SemaphoreType.DMA((n_col,)),
            ],
            compiler_params=pltpu.CompilerParams(collective_id=3, has_side_effects=True),
        )(gram)
    return pl.pallas_call(
        finish_kernel,
        out_shape=shape((vectors, width), f32),
        in_specs=[VMEM, VMEM],
        out_specs=VMEM,
        compiler_params=local_params(),
    )(product, inverse)


def solution(mesh):
    placed = (
        P("row", "col", None),
        P("row", "col"),
        P("row", "col"),
        P("row", "col"),
        P(None, ("row", "col")),
    )
    return jax.shard_map(
        functools.partial(per_device, mesh.shape["row"], mesh.shape["col"]),
        mesh=mesh,
        in_specs=placed,
        out_specs=P(None, ("row", "col")),
        check_vma=False,
    )
```

```python
import functools

import jax
import jax.numpy as jnp
from jax import lax
from jax.experimental import pallas as pl
from jax.experimental.pallas import tpu as pltpu
from jax.sharding import PartitionSpec as P

ITERS = 2
MESH = pl.DeviceIdType.MESH
ANY = pl.BlockSpec(memory_space=pl.ANY)
VMEM = pl.BlockSpec(memory_space=pltpu.VMEM)
SMEM = pl.BlockSpec(memory_space=pltpu.SMEM)
VMEM_BYTES = 48 << 20


def greet(n_row, n_col):
    my_row, my_col = lax.axis_index("row"), lax.axis_index("col")
    barrier = pltpu.get_barrier_semaphore()
    for d in range(1, n_col):
        peer = lax.rem(my_col + d, n_col)
        pl.semaphore_signal(barrier, inc=1, device_id=(my_row, peer), device_id_type=MESH)
    for d in range(1, n_row):
        peer = lax.rem(my_row + d, n_row)
        pl.semaphore_signal(barrier, inc=1, device_id=(peer, my_col), device_id_type=MESH)
    pl.semaphore_wait(barrier, n_col + n_row - 2)
    return my_row, my_col


def exchange_kernel(n_row, n_col, c_src, r_src, c_dst, r_dst, own, c_send, c_recv, r_send, r_recv):
    my_row, my_col = greet(n_row, n_col)
    shared = r_src.shape[0] == 1
    copies = []
    for d in range(1, n_row):
        peer = lax.rem(my_row + d, n_row)
        copies.append(
            pltpu.make_async_remote_copy(
                src_ref=r_src.at[0 if shared else peer],
                dst_ref=r_dst.at[my_row],
                send_sem=r_send.at[d],
                recv_sem=r_recv.at[d],
                device_id=(peer, my_col),
                device_id_type=MESH,
            )
        )
    for d in range(1, n_col):
        peer = lax.rem(my_col + d, n_col)
        copies.append(
            pltpu.make_async_remote_copy(
                src_ref=c_src.at[peer],
                dst_ref=c_dst.at[my_col],
                send_sem=c_send.at[d],
                recv_sem=c_recv.at[d],
                device_id=(my_row, peer),
                device_id_type=MESH,
            )
        )
    copies.append(pltpu.make_async_copy(c_src.at[my_col], c_dst.at[my_col], own.at[0]))
    copies.append(
        pltpu.make_async_copy(r_src.at[0 if shared else my_row], r_dst.at[my_row], own.at[1])
    )
    for copy in copies:
        copy.start()
    for copy in copies:
        copy.wait()


def exchange(n_row, n_col, collective_id, c_src, r_src):
    return pl.pallas_call(
        functools.partial(exchange_kernel, n_row, n_col),
        out_shape=(
            jax.ShapeDtypeStruct(c_src.shape, c_src.dtype),
            jax.ShapeDtypeStruct((n_row,) + r_src.shape[1:], r_src.dtype),
        ),
        in_specs=[ANY, ANY],
        out_specs=(ANY, ANY),
        scratch_shapes=[
            pltpu.SemaphoreType.DMA((2,)),
            pltpu.SemaphoreType.DMA((n_col,)),
            pltpu.SemaphoreType.DMA((n_col,)),
            pltpu.SemaphoreType.DMA((n_row,)),
            pltpu.SemaphoreType.DMA((n_row,)),
        ],
        compiler_params=pltpu.CompilerParams(collective_id=collective_id, has_side_effects=True),
    )(c_src, r_src)


def split(value):
    high = value.astype(jnp.bfloat16)
    return high, (value - high.astype(jnp.float32)).astype(jnp.bfloat16)


def inverse_stack(inverse):
    high, low = split(inverse)
    return jnp.concatenate([high, low, high, low], axis=1)


def apply_inverse(stacked, product):
    high, low = split(product)
    parts = jnp.concatenate([high, high, low, low], axis=0)
    return jnp.dot(stacked, parts, preferred_element_type=jnp.float32)


def factor_inverse(packed, size):
    full = jnp.concatenate([packed[:, size * i : size * (i + 1)] for i in range(size // 8)], axis=0)
    rows = lax.broadcasted_iota(jnp.int32, (size, size), 0)
    lanes = lax.broadcasted_iota(jnp.int32, (size, size), 1)
    work = jnp.concatenate([full, (rows == lanes).astype(jnp.float32)], axis=1)
    row_ids = lax.broadcasted_iota(jnp.int32, (size, 2 * size), 0)
    for j in range(size):
        scale = 1.0 / jnp.sqrt(work[j : j + 1, j : j + 1])
        pivot_row = work[j : j + 1, :] * scale
        factors = work[:, j : j + 1] * scale
        work = jnp.where(
            row_ids > j, work - factors * pivot_row, jnp.where(row_ids == j, pivot_row, work)
        )
    return work[:, size:]


def sum_over_mesh(n_row, n_col, gram, row_in, row_sum, col_in, r_send, r_recv, c_send, c_recv):
    my_row, my_col = lax.axis_index("row"), lax.axis_index("col")
    copies = []
    for d in range(1, n_row):
        peer = lax.rem(my_row + d, n_row)
        copies.append(
            pltpu.make_async_remote_copy(
                src_ref=gram,
                dst_ref=row_in.at[my_row],
                send_sem=r_send.at[d],
                recv_sem=r_recv.at[d],
                device_id=(peer, my_col),
                device_id_type=MESH,
            )
        )
    for copy in copies:
        copy.start()
    row_in[my_row] = gram[...]
    for copy in copies:
        copy.wait()
    row_sum[...] = jnp.sum(row_in[...], axis=0)
    copies = []
    for d in range(1, n_col):
        peer = lax.rem(my_col + d, n_col)
        copies.append(
            pltpu.make_async_remote_copy(
                src_ref=row_sum,
                dst_ref=col_in.at[my_col],
                send_sem=c_send.at[d],
                recv_sem=c_recv.at[d],
                device_id=(my_row, peer),
                device_id_type=MESH,
            )
        )
    for copy in copies:
        copy.start()
    col_in[my_col] = row_sum[...]
    for copy in copies:
        copy.wait()
    return jnp.sum(col_in[...], axis=0)


def product_kernel(first, n_row, n_col, pieces, panel, order, *refs):
    if first:
        wanted, all_cols, perm, cols, live, source, blocks = refs[:7]
        refs = refs[7:]
    else:
        wanted, all_cols, perm, cols, live, product, gram, blocks = refs[:8]
        refs = refs[8:]
    row_terms, col_terms = refs[:2]
    held, c_out, c_in, c_back, r_out, r_in, r_back, held_blocks, own = refs[2:11]
    sems = refs[11:19]
    c_send, c_recv, r_send, r_recv, cb_send, cb_recv, rb_send, rb_recv = sems
    share = c_out.shape[1]
    per_piece = n_col // pieces
    my_row, my_col = lax.axis_index("row"), lax.axis_index("col")
    base = my_row * panel

    load_blocks = pltpu.make_async_copy(blocks, held_blocks, own.at[0])
    load_blocks.start()
    if first:
        for b in range(panel):
            held[b] = source[:, b * 128 : (b + 1) * 128].astype(jnp.bfloat16)
        greet(n_row, n_col)
    else:
        product_in = refs[19]
        load_product = pltpu.make_async_copy(product, product_in, own.at[1])
        load_product.start()
        greet(n_row, n_col)
        packed = sum_over_mesh(n_row, n_col, gram, *refs[20:]) / order
        stacked = inverse_stack(factor_inverse(packed, held.shape[1]))
        load_product.wait()

        def round_block(b, carry):
            held[b] = apply_inverse(stacked, product_in[b]).astype(jnp.bfloat16)
            return carry

        lax.fori_loop(0, panel, round_block, 0, unroll=8)

    c_copies, r_copies = [None] * n_col, []
    for j in range(pieces):
        for e in range(n_row):
            p = lax.rem(my_row + e, n_row)

            for d in range(j * per_piece, (j + 1) * per_piece):
                q = lax.rem(my_col + n_col - d, n_col)

                def one_r(a, carry):
                    at = jnp.clip(all_cols[p, q * share + a] - base, 0, panel - 1)
                    target = r_in if e == 0 else r_out
                    target[p, j, (d - j * per_piece) * share + a] = held[at]
                    return carry

                lax.fori_loop(0, share, one_r, 0, unroll=share)
            if e > 0:
                copy = pltpu.make_async_remote_copy(
                    src_ref=r_out.at[p, j],
                    dst_ref=r_in.at[my_row, j],
                    send_sem=r_send.at[e, j],
                    recv_sem=r_recv.at[e, j],
                    device_id=(p, my_col),
                    device_id_type=MESH,
                )
                copy.start()
                r_copies.append((j, copy))
        for d in range(j * per_piece, (j + 1) * per_piece):
            p = lax.rem(my_col + d, n_col)
            target = c_in if d == 0 else c_out

            def one_c(a, carry):
                target[p, a] = held[wanted[p * share + a]]
                return carry

            lax.fori_loop(0, share, one_c, 0, unroll=share)
            if d > 0:
                copy = pltpu.make_async_remote_copy(
                    src_ref=c_out.at[p],
                    dst_ref=c_in.at[my_col],
                    send_sem=c_send.at[d],
                    recv_sem=c_recv.at[d],
                    device_id=(my_row, p),
                    device_id_type=MESH,
                )
                copy.start()
                c_copies[d] = copy
    load_blocks.wait()

    back = []
    for j in range(pieces):
        for piece, copy in r_copies:
            if piece == j:
                copy.wait()
        for d in range(j * per_piece, (j + 1) * per_piece):
            q = lax.rem(my_col + n_col - d, n_col)
            if d > 0:
                c_copies[d].wait()

            def one_slot(a, carry):
                t = q * share + a
                at = (d - j * per_piece) * share + a
                block = held_blocks[perm[t]]
                alive = live[t] > 0
                x_col = r_in[0, j, at]
                for p in range(1, n_row):
                    x_col = jnp.where(cols[t] // panel == p, r_in[p, j, at], x_col)
                row_product = lax.dot_general(
                    x_col, block, (((1,), (1,)), ((), ())), preferred_element_type=jnp.float32
                )
                col_product = jnp.dot(c_in[q, a], block, preferred_element_type=jnp.float32)
                c_back[q, a] = jnp.where(alive, row_product, 0.0).astype(jnp.bfloat16)
                r_back[j, at] = jnp.where(alive, col_product, 0.0).astype(jnp.bfloat16)
                return carry

            lax.fori_loop(0, share, one_slot, 0, unroll=share)
            if d == 0:
                copy = pltpu.make_async_copy(c_back.at[q], row_terms.at[my_col], own.at[2])
            else:
                copy = pltpu.make_async_remote_copy(
                    src_ref=c_back.at[q],
                    dst_ref=row_terms.at[my_col],
                    send_sem=cb_send.at[d],
                    recv_sem=cb_recv.at[d],
                    device_id=(my_row, q),
                    device_id_type=MESH,
                )
            copy.start()
            back.append(copy)
        for e in range(n_row):
            p = lax.rem(my_row + e, n_row)
            if e == 0:
                copy = pltpu.make_async_copy(
                    r_back.at[j], col_terms.at[my_row, j], own.at[3 + j]
                )
            else:
                copy = pltpu.make_async_remote_copy(
                    src_ref=r_back.at[j],
                    dst_ref=col_terms.at[my_row, j],
                    send_sem=rb_send.at[e, j],
                    recv_sem=rb_recv.at[e, j],
                    device_id=(p, my_col),
                    device_id_type=MESH,
                )
            copy.start()
            back.append(copy)
    for copy in back:
        copy.wait()


def sum_kernel(
    n_col, wanted, all_cols, row_terms, col_terms, product, gram, row_held, col_held, sem
):
    panel, vectors = product.shape[0], product.shape[1]
    share = row_terms.shape[0] // n_col
    my_row, my_col = lax.axis_index("row"), lax.axis_index("col")
    base = my_row * panel
    load_rows = pltpu.make_async_copy(row_terms, row_held, sem.at[0])
    load_cols = pltpu.make_async_copy(col_terms, col_held, sem.at[1])
    load_rows.start()
    load_cols.start()
    product[...] = jnp.zeros_like(product)
    load_rows.wait()

    def one_row(t, carry):
        at = wanted[t]
        product[at] = product[at] + row_held[t].astype(jnp.float32)
        return carry

    lax.fori_loop(0, row_held.shape[0], one_row, 0, unroll=4)
    load_cols.wait()
    for p in range(all_cols.shape[0]):

        def one_col(i, carry):
            owner = lax.rem(my_col + n_col - i // share, n_col)
            at = all_cols[p, owner * share + lax.rem(i, share)] - base

            @pl.when((at >= 0) & (at < panel))
            def _():
                product[at] = product[at] + col_held[p, i].astype(jnp.float32)

            return carry

        lax.fori_loop(0, col_held.shape[1], one_col, 0, unroll=4)

    def one_gram(b, total):
        high, low = split(product[b])
        parts = jnp.concatenate([high, low], axis=0)
        return total + lax.dot_general(
            parts, parts, (((1,), (1,)), ((), ())), preferred_element_type=jnp.float32
        )

    total = lax.fori_loop(
        0, panel, one_gram, jnp.zeros((2 * vectors, 2 * vectors), jnp.float32), unroll=8
    )
    upper = total[:vectors] + total[vectors:]
    full = upper[:, :vectors] + upper[:, vectors:]
    gram[...] = jnp.concatenate([full[8 * i : 8 * i + 8] for i in range(vectors // 8)], axis=1)


def factor_kernel(n_row, n_col, order, gram, inverse, *scratch):
    greet(n_row, n_col)
    packed = sum_over_mesh(n_row, n_col, gram, *scratch) / order
    inverse[...] = factor_inverse(packed, inverse.shape[0])


def finish_kernel(source, inverse, out):
    stacked = inverse_stack(inverse[...])
    for b in range(source.shape[0]):
        out[:, b * 128 : (b + 1) * 128] = apply_inverse(stacked, source[b])


def local_params():
    return pltpu.CompilerParams(vmem_limit_bytes=VMEM_BYTES)


def per_device(n_row, n_col, blocks, block_rows, block_cols, counts, start_vectors):
    slots, size = blocks.shape[0], blocks.shape[1]
    vectors, width = start_vectors.shape
    panel = width // size
    share = slots // n_col
    bf16, f32 = jnp.bfloat16, jnp.float32
    shape = jax.ShapeDtypeStruct

    rows, cols, ids = block_rows[0], block_cols[0], jnp.arange(slots, dtype=jnp.int32)
    owner = rows // panel
    earlier = (owner[None, :] == owner[:, None]) & (ids[None, :] < ids[:, None])
    place = owner * share + jnp.sum(earlier.astype(jnp.int32), axis=1)
    here = (place[None, :] == ids[:, None]).astype(jnp.int32)
    perm = jnp.sum(here * ids[None, :], axis=1)
    rows = jnp.sum(here * rows[None, :], axis=1)
    cols = jnp.sum(here * cols[None, :], axis=1)
    live = (perm < counts[0, 0]).astype(jnp.int32)

    row_ask = jnp.pad((rows % panel).reshape(n_col, 1, share), ((0, 0), (0, 7), (0, 128 - share)))
    col_ask = jnp.pad(cols.reshape(1, 1, slots), ((0, 0), (0, 7), (0, 128 - slots)))
    row_got, col_got = exchange(n_row, n_col, 0, row_ask, col_ask)
    wanted = row_got[:, 0, :share].reshape(slots)
    all_cols = col_got[:, 0, :slots]

    gram_shape = (8, vectors * vectors // 8)
    pieces = 4 if n_col % 4 == 0 else 1
    dma = pltpu.SemaphoreType.DMA
    order = float(n_row * n_col * width)
    mesh_sum = [
        pltpu.VMEM((n_row,) + gram_shape, f32),
        pltpu.VMEM(gram_shape, f32),
        pltpu.VMEM((n_col,) + gram_shape, f32),
        dma((n_row,)),
        dma((n_row,)),
        dma((n_col,)),
        dma((n_col,)),
    ]
    by_owner = (n_col, share, vectors, size)
    by_piece = (pieces, slots // pieces, vectors, size)
    product = gram = None
    for iteration in range(ITERS):
        first = iteration == 0
        sources = (start_vectors,) if first else (product, gram)
        row_terms, col_terms = pl.pallas_call(
            functools.partial(product_kernel, first, n_row, n_col, pieces, panel, order),
            out_shape=(shape(by_owner, bf16), shape((n_row,) + by_piece, bf16)),
            in_specs=[SMEM] * 5 + ([VMEM] if first else [ANY, VMEM]) + [ANY],
            out_specs=(ANY, ANY),
            scratch_shapes=[
                pltpu.VMEM((panel, vectors, size), bf16),
                pltpu.VMEM(by_owner, bf16),
                pltpu.VMEM(by_owner, bf16),
                pltpu.VMEM(by_owner, bf16),
                pltpu.VMEM((n_row,) + by_piece, bf16),
                pltpu.VMEM((n_row,) + by_piece, bf16),
                pltpu.VMEM(by_piece, bf16),
                pltpu.VMEM(blocks.shape, bf16),
                dma((3 + pieces,)),
                dma((n_col,)),
                dma((n_col,)),
                dma((n_row, pieces)),
                dma((n_row, pieces)),
                dma((n_col,)),
                dma((n_col,)),
                dma((n_row, pieces)),
                dma((n_row, pieces)),
            ]
            + ([] if first else [pltpu.VMEM((panel, vectors, size), f32)] + mesh_sum),
            compiler_params=pltpu.CompilerParams(
                collective_id=1 if first else 2,
                has_side_effects=True,
                vmem_limit_bytes=VMEM_BYTES,
            ),
        )(wanted, all_cols, perm, cols, live, *sources, blocks)
        product, gram = pl.pallas_call(
            functools.partial(sum_kernel, n_col),
            out_shape=(shape((panel, vectors, size), f32), shape(gram_shape, f32)),
            in_specs=[SMEM, SMEM, ANY, ANY],
            out_specs=(VMEM, VMEM),
            scratch_shapes=[
                pltpu.VMEM((slots, vectors, size), bf16),
                pltpu.VMEM((n_row, slots, vectors, size), bf16),
                dma((2,)),
            ],
            compiler_params=local_params(),
        )(
            wanted,
            all_cols,
            row_terms.reshape(slots, vectors, size),
            col_terms.reshape(n_row, slots, vectors, size),
        )
    inverse = pl.pallas_call(
        functools.partial(factor_kernel, n_row, n_col, order),
        out_shape=shape((vectors, vectors), f32),
        in_specs=[VMEM],
        out_specs=VMEM,
        scratch_shapes=mesh_sum,
        compiler_params=pltpu.CompilerParams(collective_id=3, has_side_effects=True),
    )(gram)
    return pl.pallas_call(
        finish_kernel,
        out_shape=shape((vectors, width), f32),
        in_specs=[VMEM, VMEM],
        out_specs=VMEM,
        compiler_params=local_params(),
    )(product, inverse)


def solution(mesh):
    placed = (
        P("row", "col", None),
        P("row", "col"),
        P("row", "col"),
        P("row", "col"),
        P(None, ("row", "col")),
    )
    return jax.shard_map(
        functools.partial(per_device, mesh.shape["row"], mesh.shape["col"]),
        mesh=mesh,
        in_specs=placed,
        out_specs=P(None, ("row", "col")),
        check_vma=False,
    )
```

```python
import functools

import jax
import jax.numpy as jnp
from jax import lax
from jax.experimental import pallas as pl
from jax.experimental.pallas import tpu as pltpu
from jax.sharding import PartitionSpec as P

ITERS = 2
MESH = pl.DeviceIdType.MESH
HBM = pl.BlockSpec(memory_space=pltpu.HBM)
VMEM = pl.BlockSpec(memory_space=pltpu.VMEM)
SMEM = pl.BlockSpec(memory_space=pltpu.SMEM)
VMEM_BYTES = 48 << 20


def greet(n_row, n_col):
    my_row, my_col = lax.axis_index("row"), lax.axis_index("col")
    barrier = pltpu.get_barrier_semaphore()
    for d in range(1, n_col):
        peer = lax.rem(my_col + d, n_col)
        pl.semaphore_signal(barrier, inc=1, device_id=(my_row, peer), device_id_type=MESH)
    for d in range(1, n_row):
        peer = lax.rem(my_row + d, n_row)
        pl.semaphore_signal(barrier, inc=1, device_id=(peer, my_col), device_id_type=MESH)
    pl.semaphore_wait(barrier, n_col + n_row - 2)
    return my_row, my_col


def split(value):
    high = value.astype(jnp.bfloat16)
    return high, (value - high.astype(jnp.float32)).astype(jnp.bfloat16)


def inverse_stack(inverse):
    high, low = split(inverse)
    return jnp.concatenate([high, low, high, low], axis=1)


def pair(blocks, i):
    return jnp.concatenate([blocks[2 * i], blocks[2 * i + 1]], axis=1)


def apply_inverse(stacked, product):
    high, low = split(product)
    parts = jnp.concatenate([high, high, low, low], axis=0)
    return jnp.dot(stacked, parts, preferred_element_type=jnp.float32)


def factor_inverse(packed, size):
    full = jnp.concatenate([packed[:, size * i : size * (i + 1)] for i in range(size // 8)], axis=0)
    rows = lax.broadcasted_iota(jnp.int32, (size, size), 0)
    lanes = lax.broadcasted_iota(jnp.int32, (size, size), 1)
    work = jnp.concatenate([full, (rows == lanes).astype(jnp.float32)], axis=1)
    row_ids = lax.broadcasted_iota(jnp.int32, (size, 1), 0)
    for j in range(size):
        factors = work[:, j : j + 1] * (1.0 / work[j : j + 1, j : j + 1])
        work = work - jnp.where(row_ids > j, factors, 0.0) * work[j : j + 1, :]
    pivots = jnp.sum(jnp.where(rows == lanes, work[:, :size], 0.0), axis=1, keepdims=True)
    return work[:, size:] * (1.0 / jnp.sqrt(pivots))


def sum_over_mesh(n_row, n_col, gram, row_in, row_sum, col_in, r_send, r_recv, c_send, c_recv):
    my_row, my_col = lax.axis_index("row"), lax.axis_index("col")
    copies = []
    for d in range(1, n_row):
        peer = lax.rem(my_row + d, n_row)
        copies.append(
            pltpu.make_async_remote_copy(
                src_ref=gram,
                dst_ref=row_in.at[my_row],
                send_sem=r_send.at[d],
                recv_sem=r_recv.at[d],
                device_id=(peer, my_col),
                device_id_type=MESH,
            )
        )
    for copy in copies:
        copy.start()
    row_in[my_row] = gram[...]
    for copy in copies:
        copy.wait()
    row_sum[...] = jnp.sum(row_in[...], axis=0)
    copies = []
    for d in range(1, n_col):
        peer = lax.rem(my_col + d, n_col)
        copies.append(
            pltpu.make_async_remote_copy(
                src_ref=row_sum,
                dst_ref=col_in.at[my_col],
                send_sem=c_send.at[d],
                recv_sem=c_recv.at[d],
                device_id=(my_row, peer),
                device_id_type=MESH,
            )
        )
    for copy in copies:
        copy.start()
    col_in[my_col] = row_sum[...]
    for copy in copies:
        copy.wait()
    return jnp.sum(col_in[...], axis=0)


def product_kernel(first, n_row, n_col, pieces, panel, order, *refs):
    if first:
        row_ask, col_ask, perm, cols, live, source, blocks = refs[:7]
        wanted_out, all_cols_out = refs[7:9]
        refs = refs[9:]
    else:
        wanted, all_cols, perm, cols, live, product, gram, blocks = refs[:8]
        refs = refs[8:]
    row_terms, col_terms = refs[:2]
    held, c_out, c_in, c_back, r_out, r_in, r_back, held_blocks, own = refs[2:11]
    sems = refs[11:19]
    c_send, c_recv, r_send, r_recv, cb_send, cb_recv, rb_send, rb_recv = sems
    share = c_out.shape[1]
    per_piece = n_col // pieces
    my_row, my_col = lax.axis_index("row"), lax.axis_index("col")
    base = my_row * panel

    load_blocks = pltpu.make_async_copy(blocks, held_blocks, own.at[0])
    load_blocks.start()
    if first:
        source_in, wanted, all_cols, asked, ac_send, ac_recv, ar_send, ar_recv = refs[19:]
        load_source = pltpu.make_async_copy(source, source_in, own.at[1])
        load_source.start()
        greet(n_row, n_col)
        asks = [
            pltpu.make_async_copy(row_ask.at[my_col], wanted_out.at[my_col], asked.at[0]),
            pltpu.make_async_copy(col_ask.at[0], all_cols_out.at[my_row], asked.at[1]),
        ]
        for d in range(1, n_row):
            peer = lax.rem(my_row + d, n_row)
            asks.append(
                pltpu.make_async_remote_copy(
                    src_ref=col_ask.at[0],
                    dst_ref=all_cols_out.at[my_row],
                    send_sem=ar_send.at[d],
                    recv_sem=ar_recv.at[d],
                    device_id=(peer, my_col),
                    device_id_type=MESH,
                )
            )
        for d in range(1, n_col):
            peer = lax.rem(my_col + d, n_col)
            asks.append(
                pltpu.make_async_remote_copy(
                    src_ref=row_ask.at[peer],
                    dst_ref=wanted_out.at[my_col],
                    send_sem=ac_send.at[d],
                    recv_sem=ac_recv.at[d],
                    device_id=(my_row, peer),
                    device_id_type=MESH,
                )
            )
        for copy in asks:
            copy.start()
        load_source.wait()
        for b in range(panel):
            held[b] = source_in[:, b * 128 : (b + 1) * 128].astype(jnp.bfloat16)
        for copy in asks:
            copy.wait()
        lists = [
            pltpu.make_async_copy(wanted_out, wanted, asked.at[2]),
            pltpu.make_async_copy(all_cols_out, all_cols, asked.at[3]),
        ]
        for copy in lists:
            copy.start()
        for copy in lists:
            copy.wait()
    else:
        product_in = refs[19]
        load_product = pltpu.make_async_copy(product, product_in, own.at[1])
        load_product.start()
        greet(n_row, n_col)
        packed = sum_over_mesh(n_row, n_col, gram, *refs[20:]) / order
        stacked = inverse_stack(factor_inverse(packed, held.shape[1]))
        load_product.wait()

        def round_blocks(i, carry):
            both = apply_inverse(stacked, pair(product_in, i)).astype(jnp.bfloat16)
            held[2 * i] = both[:, :128]
            held[2 * i + 1] = both[:, 128:]
            return carry

        lax.fori_loop(0, panel // 2, round_blocks, 0, unroll=8)

    c_copies, r_copies = [None] * n_col, []
    for j in range(pieces):
        for e in range(n_row):
            p = lax.rem(my_row + e, n_row)

            for d in range(j * per_piece, (j + 1) * per_piece):
                q = lax.rem(my_col + n_col - d, n_col)

                def one_r(a, carry):
                    at = jnp.clip(all_cols[p, 0, q * share + a] - base, 0, panel - 1)
                    target = r_in if e == 0 else r_out
                    target[p, j, (d - j * per_piece) * share + a] = held[at]
                    return carry

                lax.fori_loop(0, share, one_r, 0, unroll=share)
            if e > 0:
                copy = pltpu.make_async_remote_copy(
                    src_ref=r_out.at[p, j],
                    dst_ref=r_in.at[my_row, j],
                    send_sem=r_send.at[e, j],
                    recv_sem=r_recv.at[e, j],
                    device_id=(p, my_col),
                    device_id_type=MESH,
                )
                copy.start()
                r_copies.append((j, copy))
        for d in range(j * per_piece, (j + 1) * per_piece):
            p = lax.rem(my_col + d, n_col)
            target = c_in if d == 0 else c_out

            def one_c(a, carry):
                target[p, a] = held[wanted[p, 0, a]]
                return carry

            lax.fori_loop(0, share, one_c, 0, unroll=share)
            if d > 0:
                copy = pltpu.make_async_remote_copy(
                    src_ref=c_out.at[p],
                    dst_ref=c_in.at[my_col],
                    send_sem=c_send.at[d],
                    recv_sem=c_recv.at[d],
                    device_id=(my_row, p),
                    device_id_type=MESH,
                )
                copy.start()
                c_copies[d] = copy
    load_blocks.wait()

    back = []
    for j in range(pieces):
        for piece, copy in r_copies:
            if piece == j:
                copy.wait()
        for d in range(j * per_piece, (j + 1) * per_piece):
            q = lax.rem(my_col + n_col - d, n_col)
            if d > 0:
                c_copies[d].wait()

            def one_slot(a, carry):
                t = q * share + a
                at = (d - j * per_piece) * share + a
                block = held_blocks[perm[t]]
                alive = live[t] > 0
                x_col = r_in[0, j, at]
                for p in range(1, n_row):
                    x_col = jnp.where(cols[t] // panel == p, r_in[p, j, at], x_col)
                row_product = lax.dot_general(
                    x_col, block, (((1,), (1,)), ((), ())), preferred_element_type=jnp.float32
                )
                col_product = jnp.dot(c_in[q, a], block, preferred_element_type=jnp.float32)
                c_back[q, a] = jnp.where(alive, row_product, 0.0).astype(jnp.bfloat16)
                r_back[j, at] = jnp.where(alive, col_product, 0.0).astype(jnp.bfloat16)
                return carry

            lax.fori_loop(0, share, one_slot, 0, unroll=share)
            if d == 0:
                copy = pltpu.make_async_copy(c_back.at[q], row_terms.at[my_col], own.at[2])
            else:
                copy = pltpu.make_async_remote_copy(
                    src_ref=c_back.at[q],
                    dst_ref=row_terms.at[my_col],
                    send_sem=cb_send.at[d],
                    recv_sem=cb_recv.at[d],
                    device_id=(my_row, q),
                    device_id_type=MESH,
                )
            copy.start()
            back.append(copy)
        for e in range(n_row):
            p = lax.rem(my_row + e, n_row)
            if e == 0:
                copy = pltpu.make_async_copy(
                    r_back.at[j], col_terms.at[my_row, j], own.at[3 + j]
                )
            else:
                copy = pltpu.make_async_remote_copy(
                    src_ref=r_back.at[j],
                    dst_ref=col_terms.at[my_row, j],
                    send_sem=rb_send.at[e, j],
                    recv_sem=rb_recv.at[e, j],
                    device_id=(p, my_col),
                    device_id_type=MESH,
                )
            copy.start()
            back.append(copy)
    for copy in back:
        copy.wait()


def sum_kernel(
    n_col, wanted, all_cols, row_terms, col_terms, product, gram, row_held, col_held, sem
):
    panel, vectors = product.shape[0], product.shape[1]
    share = row_terms.shape[0] // n_col
    my_row, my_col = lax.axis_index("row"), lax.axis_index("col")
    base = my_row * panel
    load_rows = pltpu.make_async_copy(row_terms, row_held, sem.at[0])
    load_cols = pltpu.make_async_copy(col_terms, col_held, sem.at[1])
    load_rows.start()
    load_cols.start()
    product[...] = jnp.zeros_like(product)
    load_rows.wait()

    def one_owner(q, carry):
        for a in range(share):
            at = wanted[q, 0, a]
            product[at] = product[at] + row_held[q * share + a].astype(jnp.float32)
        return carry

    lax.fori_loop(0, n_col, one_owner, 0, unroll=2)
    load_cols.wait()
    for p in range(all_cols.shape[0]):

        def one_piece(d, carry):
            owner = lax.rem(my_col + n_col - d, n_col)
            for a in range(share):
                at = all_cols[p, 0, owner * share + a] - base
                term = col_held[p, d * share + a].astype(jnp.float32)
                term = jnp.where((at >= 0) & (at < panel), term, 0.0)
                at = jnp.clip(at, 0, panel - 1)
                product[at] = product[at] + term
            return carry

        lax.fori_loop(0, n_col, one_piece, 0, unroll=2)

    def one_gram(i, total):
        high, low = split(pair(product, i))
        parts = jnp.concatenate([high, low], axis=0)
        return total + lax.dot_general(
            parts, parts, (((1,), (1,)), ((), ())), preferred_element_type=jnp.float32
        )

    total = lax.fori_loop(
        0, panel // 2, one_gram, jnp.zeros((2 * vectors, 2 * vectors), jnp.float32), unroll=8
    )
    upper = total[:vectors] + total[vectors:]
    full = upper[:, :vectors] + upper[:, vectors:]
    gram[...] = jnp.concatenate([full[8 * i : 8 * i + 8] for i in range(vectors // 8)], axis=1)


def factor_kernel(n_row, n_col, order, gram, inverse, *scratch):
    greet(n_row, n_col)
    packed = sum_over_mesh(n_row, n_col, gram, *scratch) / order
    inverse[...] = factor_inverse(packed, inverse.shape[0])


def finish_kernel(source, inverse, out):
    stacked = inverse_stack(inverse[...])
    for i in range(source.shape[0] // 2):
        out[:, i * 256 : (i + 1) * 256] = apply_inverse(stacked, pair(source, i))


def local_params():
    return pltpu.CompilerParams(vmem_limit_bytes=VMEM_BYTES)


def per_device(n_row, n_col, blocks, block_rows, block_cols, counts, start_vectors):
    slots, size = blocks.shape[0], blocks.shape[1]
    vectors, width = start_vectors.shape
    panel = width // size
    share = slots // n_col
    bf16, f32 = jnp.bfloat16, jnp.float32
    shape = jax.ShapeDtypeStruct

    rows, cols, ids = block_rows[0], block_cols[0], jnp.arange(slots, dtype=jnp.int32)
    owner = rows // panel
    earlier = (owner[None, :] == owner[:, None]) & (ids[None, :] < ids[:, None])
    place = owner * share + jnp.sum(earlier.astype(jnp.int32), axis=1)
    here = (place[None, :] == ids[:, None]).astype(jnp.int32)
    perm = jnp.sum(here * ids[None, :], axis=1)
    rows = jnp.sum(here * rows[None, :], axis=1)
    cols = jnp.sum(here * cols[None, :], axis=1)
    live = (perm < counts[0, 0]).astype(jnp.int32)

    row_ask = jnp.pad((rows % panel).reshape(n_col, 1, share), ((0, 0), (0, 0), (0, 128 - share)))
    col_ask = jnp.pad(cols.reshape(1, 1, slots), ((0, 0), (0, 0), (0, 128 - slots)))
    gram_shape = (8, vectors * vectors // 8)
    pieces = 4 if n_col % 4 == 0 else 1
    dma = pltpu.SemaphoreType.DMA
    order = float(n_row * n_col * width)
    mesh_sum = [
        pltpu.VMEM((n_row,) + gram_shape, f32),
        pltpu.VMEM(gram_shape, f32),
        pltpu.VMEM((n_col,) + gram_shape, f32),
        dma((n_row,)),
        dma((n_row,)),
        dma((n_col,)),
        dma((n_col,)),
    ]
    by_owner = (n_col, share, vectors, size)
    by_piece = (pieces, slots // pieces, vectors, size)
    product = gram = None
    for iteration in range(ITERS):
        first = iteration == 0
        if first:
            lists, sources = (row_ask, col_ask), (start_vectors,)
            list_shapes = (shape((n_col, 1, 128), jnp.int32), shape((n_row, 1, 128), jnp.int32))
        else:
            lists, sources, list_shapes = (wanted, all_cols), (product, gram), ()
        *got, row_terms, col_terms = pl.pallas_call(
            functools.partial(product_kernel, first, n_row, n_col, pieces, panel, order),
            out_shape=list_shapes + (shape(by_owner, bf16), shape((n_row,) + by_piece, bf16)),
            in_specs=([HBM] if first else [SMEM]) * 2
            + [SMEM] * 3
            + ([HBM] if first else [HBM, VMEM])
            + [HBM],
            out_specs=(HBM,) * (len(list_shapes) + 2),
            scratch_shapes=[
                pltpu.VMEM((panel, vectors, size), bf16),
                pltpu.VMEM(by_owner, bf16),
                pltpu.VMEM(by_owner, bf16),
                pltpu.VMEM(by_owner, bf16),
                pltpu.VMEM((n_row,) + by_piece, bf16),
                pltpu.VMEM((n_row,) + by_piece, bf16),
                pltpu.VMEM(by_piece, bf16),
                pltpu.VMEM(blocks.shape, bf16),
                dma((3 + pieces,)),
                dma((n_col,)),
                dma((n_col,)),
                dma((n_row, pieces)),
                dma((n_row, pieces)),
                dma((n_col,)),
                dma((n_col,)),
                dma((n_row, pieces)),
                dma((n_row, pieces)),
            ]
            + (
                [
                    pltpu.VMEM((vectors, width), f32),
                    pltpu.SMEM((n_col, 1, 128), jnp.int32),
                    pltpu.SMEM((n_row, 1, 128), jnp.int32),
                    dma((4,)),
                    dma((n_col,)),
                    dma((n_col,)),
                    dma((n_row,)),
                    dma((n_row,)),
                ]
                if first
                else [pltpu.VMEM((panel, vectors, size), f32)] + mesh_sum
            ),
            compiler_params=pltpu.CompilerParams(
                collective_id=1 if first else 2,
                has_side_effects=True,
                vmem_limit_bytes=VMEM_BYTES,
            ),
        )(*lists, perm, cols, live, *sources, blocks)
        if first:
            wanted, all_cols = got
        product, gram = pl.pallas_call(
            functools.partial(sum_kernel, n_col),
            out_shape=(shape((panel, vectors, size), f32), shape(gram_shape, f32)),
            in_specs=[SMEM, SMEM, HBM, HBM],
            out_specs=(VMEM, VMEM),
            scratch_shapes=[
                pltpu.VMEM((slots, vectors, size), bf16),
                pltpu.VMEM((n_row, slots, vectors, size), bf16),
                dma((2,)),
            ],
            compiler_params=local_params(),
        )(
            wanted,
            all_cols,
            row_terms.reshape(slots, vectors, size),
            col_terms.reshape(n_row, slots, vectors, size),
        )
    inverse = pl.pallas_call(
        functools.partial(factor_kernel, n_row, n_col, order),
        out_shape=shape((vectors, vectors), f32),
        in_specs=[VMEM],
        out_specs=VMEM,
        scratch_shapes=mesh_sum,
        compiler_params=pltpu.CompilerParams(collective_id=3, has_side_effects=True),
    )(gram)
    return pl.pallas_call(
        finish_kernel,
        out_shape=shape((vectors, width), f32),
        in_specs=[VMEM, VMEM],
        out_specs=VMEM,
        compiler_params=local_params(),
    )(product, inverse)


def solution(mesh):
    placed = (
        P("row", "col", None),
        P("row", "col"),
        P("row", "col"),
        P("row", "col"),
        P(None, ("row", "col")),
    )
    return jax.shard_map(
        functools.partial(per_device, mesh.shape["row"], mesh.shape["col"]),
        mesh=mesh,
        in_specs=placed,
        out_specs=P(None, ("row", "col")),
        check_vma=False,
    )
```

```python
import functools

import jax
import jax.numpy as jnp
from jax import lax
from jax.experimental import pallas as pl
from jax.experimental.pallas import tpu as pltpu
from jax.sharding import PartitionSpec as P

ITERS = 2
MESH = pl.DeviceIdType.MESH
HBM = pl.BlockSpec(memory_space=pltpu.HBM)
VMEM = pl.BlockSpec(memory_space=pltpu.VMEM)
SMEM = pl.BlockSpec(memory_space=pltpu.SMEM)
VMEM_BYTES = 48 << 20


def greet(n_row, n_col):
    my_row, my_col = lax.axis_index("row"), lax.axis_index("col")
    barrier = pltpu.get_barrier_semaphore()
    for d in range(1, n_col):
        peer = lax.rem(my_col + d, n_col)
        pl.semaphore_signal(barrier, inc=1, device_id=(my_row, peer), device_id_type=MESH)
    for d in range(1, n_row):
        peer = lax.rem(my_row + d, n_row)
        pl.semaphore_signal(barrier, inc=1, device_id=(peer, my_col), device_id_type=MESH)
    pl.semaphore_wait(barrier, n_col + n_row - 2)
    return my_row, my_col


def split(value):
    high = value.astype(jnp.bfloat16)
    return high, (value - high.astype(jnp.float32)).astype(jnp.bfloat16)


def inverse_stack(inverse):
    high, low = split(inverse)
    return jnp.concatenate([high, low, high, low], axis=1)


def pair(blocks, i):
    return jnp.concatenate([blocks[2 * i], blocks[2 * i + 1]], axis=1)


def apply_inverse(stacked, product):
    high, low = split(product)
    parts = jnp.concatenate([high, high, low, low], axis=0)
    return jnp.dot(stacked, parts, preferred_element_type=jnp.float32)


def factor_inverse(packed, size):
    full = jnp.concatenate([packed[:, size * i : size * (i + 1)] for i in range(size // 8)], axis=0)
    rows = lax.broadcasted_iota(jnp.int32, (size, size), 0)
    lanes = lax.broadcasted_iota(jnp.int32, (size, size), 1)
    work = jnp.concatenate([full, (rows == lanes).astype(jnp.float32)], axis=1)
    row_ids = lax.broadcasted_iota(jnp.int32, work.shape, 0)
    for j in range(size):
        column = jnp.broadcast_to(work[:, j : j + 1], work.shape)
        pivot_row = work[j : j + 1, :] * (1.0 / column[j : j + 1, :])
        work = work - jnp.where(row_ids > j, column, 0.0) * pivot_row
    pivots = jnp.sum(jnp.where(rows == lanes, work[:, :size], 0.0), axis=1, keepdims=True)
    return work[:, size:] * (1.0 / jnp.sqrt(pivots))


def sum_over_mesh(n_row, n_col, gram, row_in, row_sum, col_in, r_send, r_recv, c_send, c_recv):
    my_row, my_col = lax.axis_index("row"), lax.axis_index("col")
    copies = []
    for d in range(1, n_row):
        peer = lax.rem(my_row + d, n_row)
        copies.append(
            pltpu.make_async_remote_copy(
                src_ref=gram,
                dst_ref=row_in.at[my_row],
                send_sem=r_send.at[d],
                recv_sem=r_recv.at[d],
                device_id=(peer, my_col),
                device_id_type=MESH,
            )
        )
    for copy in copies:
        copy.start()
    row_in[my_row] = gram[...]
    for copy in copies:
        copy.wait()
    row_sum[...] = jnp.sum(row_in[...], axis=0)
    copies = []
    for d in range(1, n_col):
        peer = lax.rem(my_col + d, n_col)
        copies.append(
            pltpu.make_async_remote_copy(
                src_ref=row_sum,
                dst_ref=col_in.at[my_col],
                send_sem=c_send.at[d],
                recv_sem=c_recv.at[d],
                device_id=(my_row, peer),
                device_id_type=MESH,
            )
        )
    for copy in copies:
        copy.start()
    col_in[my_col] = row_sum[...]
    for copy in copies:
        copy.wait()
    return jnp.sum(col_in[...], axis=0)


def product_kernel(first, n_row, n_col, pieces, panel, order, *refs):
    if first:
        row_ask, col_ask, perm, cols, live, source, blocks = refs[:7]
        wanted_out, all_cols_out = refs[7:9]
        refs = refs[9:]
    else:
        wanted, all_cols, perm, cols, live, product, gram, blocks = refs[:8]
        refs = refs[8:]
    row_terms, col_terms = refs[:2]
    held, c_out, c_in, c_back, r_out, r_in, r_back, held_blocks, own = refs[2:11]
    sems = refs[11:19]
    c_send, c_recv, r_send, r_recv, cb_send, cb_recv, rb_send, rb_recv = sems
    share = c_out.shape[1]
    per_piece = n_col // pieces
    my_row, my_col = lax.axis_index("row"), lax.axis_index("col")
    base = my_row * panel

    load_blocks = pltpu.make_async_copy(blocks, held_blocks, own.at[0])
    load_blocks.start()
    if first:
        source_in, wanted, all_cols, asked, ac_send, ac_recv, ar_send, ar_recv = refs[19:]
        load_source = pltpu.make_async_copy(source, source_in, own.at[1])
        load_source.start()
        greet(n_row, n_col)
        asks = [
            pltpu.make_async_copy(row_ask.at[my_col], wanted_out.at[my_col], asked.at[0]),
            pltpu.make_async_copy(col_ask.at[0], all_cols_out.at[my_row], asked.at[1]),
        ]
        for d in range(1, n_row):
            peer = lax.rem(my_row + d, n_row)
            asks.append(
                pltpu.make_async_remote_copy(
                    src_ref=col_ask.at[0],
                    dst_ref=all_cols_out.at[my_row],
                    send_sem=ar_send.at[d],
                    recv_sem=ar_recv.at[d],
                    device_id=(peer, my_col),
                    device_id_type=MESH,
                )
            )
        for d in range(1, n_col):
            peer = lax.rem(my_col + d, n_col)
            asks.append(
                pltpu.make_async_remote_copy(
                    src_ref=row_ask.at[peer],
                    dst_ref=wanted_out.at[my_col],
                    send_sem=ac_send.at[d],
                    recv_sem=ac_recv.at[d],
                    device_id=(my_row, peer),
                    device_id_type=MESH,
                )
            )
        for copy in asks:
            copy.start()
        load_source.wait()
        for b in range(panel):
            held[b] = source_in[:, b * 128 : (b + 1) * 128].astype(jnp.bfloat16)
        for copy in asks:
            copy.wait()
        lists = [
            pltpu.make_async_copy(wanted_out, wanted, asked.at[2]),
            pltpu.make_async_copy(all_cols_out, all_cols, asked.at[3]),
        ]
        for copy in lists:
            copy.start()
        for copy in lists:
            copy.wait()
    else:
        product_in = refs[19]
        load_product = pltpu.make_async_copy(product, product_in, own.at[1])
        load_product.start()
        greet(n_row, n_col)
        packed = sum_over_mesh(n_row, n_col, gram, *refs[20:]) / order
        stacked = inverse_stack(factor_inverse(packed, held.shape[1]))
        load_product.wait()

        def round_blocks(i, carry):
            both = apply_inverse(stacked, pair(product_in, i)).astype(jnp.bfloat16)
            held[2 * i] = both[:, :128]
            held[2 * i + 1] = both[:, 128:]
            return carry

        lax.fori_loop(0, panel // 2, round_blocks, 0, unroll=8)

    c_copies, r_copies = [None] * n_col, []
    for j in range(pieces):
        for e in range(n_row):
            p = lax.rem(my_row + e, n_row)

            for d in range(j * per_piece, (j + 1) * per_piece):
                q = lax.rem(my_col + n_col - d, n_col)

                def one_r(a, carry):
                    at = jnp.clip(all_cols[p, 0, q * share + a] - base, 0, panel - 1)
                    target = r_in if e == 0 else r_out
                    target[p, j, (d - j * per_piece) * share + a] = held[at]
                    return carry

                lax.fori_loop(0, share, one_r, 0, unroll=share)
            if e > 0:
                copy = pltpu.make_async_remote_copy(
                    src_ref=r_out.at[p, j],
                    dst_ref=r_in.at[my_row, j],
                    send_sem=r_send.at[e, j],
                    recv_sem=r_recv.at[e, j],
                    device_id=(p, my_col),
                    device_id_type=MESH,
                )
                copy.start()
                r_copies.append((j, copy))
        for d in range(j * per_piece, (j + 1) * per_piece):
            p = lax.rem(my_col + d, n_col)
            target = c_in if d == 0 else c_out

            def one_c(a, carry):
                target[p, a] = held[wanted[p, 0, a]]
                return carry

            lax.fori_loop(0, share, one_c, 0, unroll=share)
            if d > 0:
                copy = pltpu.make_async_remote_copy(
                    src_ref=c_out.at[p],
                    dst_ref=c_in.at[my_col],
                    send_sem=c_send.at[d],
                    recv_sem=c_recv.at[d],
                    device_id=(my_row, p),
                    device_id_type=MESH,
                )
                copy.start()
                c_copies[d] = copy
    load_blocks.wait()

    back = []
    for j in range(pieces):
        for piece, copy in r_copies:
            if piece == j:
                copy.wait()
        for d in range(j * per_piece, (j + 1) * per_piece):
            q = lax.rem(my_col + n_col - d, n_col)
            if d > 0:
                c_copies[d].wait()

            def one_slot(a, carry):
                t = q * share + a
                at = (d - j * per_piece) * share + a
                block = held_blocks[perm[t]]
                alive = live[t] > 0
                x_col = r_in[0, j, at]
                for p in range(1, n_row):
                    x_col = jnp.where(cols[t] // panel == p, r_in[p, j, at], x_col)
                row_product = lax.dot_general(
                    x_col, block, (((1,), (1,)), ((), ())), preferred_element_type=jnp.float32
                )
                col_product = jnp.dot(c_in[q, a], block, preferred_element_type=jnp.float32)
                c_back[q, a] = jnp.where(alive, row_product, 0.0).astype(jnp.bfloat16)
                r_back[j, at] = jnp.where(alive, col_product, 0.0).astype(jnp.bfloat16)
                return carry

            lax.fori_loop(0, share, one_slot, 0, unroll=share)
            if d == 0:
                copy = pltpu.make_async_copy(c_back.at[q], row_terms.at[my_col], own.at[2])
            else:
                copy = pltpu.make_async_remote_copy(
                    src_ref=c_back.at[q],
                    dst_ref=row_terms.at[my_col],
                    send_sem=cb_send.at[d],
                    recv_sem=cb_recv.at[d],
                    device_id=(my_row, q),
                    device_id_type=MESH,
                )
            copy.start()
            back.append(copy)
        for e in range(n_row):
            p = lax.rem(my_row + e, n_row)
            if e == 0:
                copy = pltpu.make_async_copy(
                    r_back.at[j], col_terms.at[my_row, j], own.at[3 + j]
                )
            else:
                copy = pltpu.make_async_remote_copy(
                    src_ref=r_back.at[j],
                    dst_ref=col_terms.at[my_row, j],
                    send_sem=rb_send.at[e, j],
                    recv_sem=rb_recv.at[e, j],
                    device_id=(p, my_col),
                    device_id_type=MESH,
                )
            copy.start()
            back.append(copy)
    for copy in back:
        copy.wait()


def sum_kernel(
    n_col, wanted, all_cols, row_terms, col_terms, product, gram, row_held, col_held, sem
):
    panel, vectors = product.shape[0], product.shape[1]
    share = row_terms.shape[0] // n_col
    my_row, my_col = lax.axis_index("row"), lax.axis_index("col")
    base = my_row * panel
    load_rows = pltpu.make_async_copy(row_terms, row_held, sem.at[0])
    load_cols = pltpu.make_async_copy(col_terms, col_held, sem.at[1])
    load_rows.start()
    load_cols.start()
    product[...] = jnp.zeros_like(product)
    load_rows.wait()

    def one_owner(q, carry):
        for a in range(share):
            at = wanted[q, 0, a]
            product[at] = product[at] + row_held[q * share + a].astype(jnp.float32)
        return carry

    lax.fori_loop(0, n_col, one_owner, 0, unroll=2)
    load_cols.wait()
    for p in range(all_cols.shape[0]):

        def one_piece(d, carry):
            owner = lax.rem(my_col + n_col - d, n_col)
            for a in range(share):
                at = all_cols[p, 0, owner * share + a] - base
                term = col_held[p, d * share + a].astype(jnp.float32)
                term = jnp.where((at >= 0) & (at < panel), term, 0.0)
                at = jnp.clip(at, 0, panel - 1)
                product[at] = product[at] + term
            return carry

        lax.fori_loop(0, n_col, one_piece, 0, unroll=2)

    def one_gram(i, total):
        high, low = split(pair(product, i))
        parts = jnp.concatenate([high, low], axis=0)
        return total + lax.dot_general(
            parts, parts, (((1,), (1,)), ((), ())), preferred_element_type=jnp.float32
        )

    total = lax.fori_loop(
        0, panel // 2, one_gram, jnp.zeros((2 * vectors, 2 * vectors), jnp.float32), unroll=8
    )
    upper = total[:vectors] + total[vectors:]
    full = upper[:, :vectors] + upper[:, vectors:]
    gram[...] = jnp.concatenate([full[8 * i : 8 * i + 8] for i in range(vectors // 8)], axis=1)


def factor_kernel(n_row, n_col, order, gram, inverse, *scratch):
    greet(n_row, n_col)
    packed = sum_over_mesh(n_row, n_col, gram, *scratch) / order
    inverse[...] = factor_inverse(packed, inverse.shape[0])


def finish_kernel(source, inverse, out):
    stacked = inverse_stack(inverse[...])
    for i in range(source.shape[0] // 2):
        out[:, i * 256 : (i + 1) * 256] = apply_inverse(stacked, pair(source, i))


def local_params():
    return pltpu.CompilerParams(vmem_limit_bytes=VMEM_BYTES)


def per_device(n_row, n_col, blocks, block_rows, block_cols, counts, start_vectors):
    slots, size = blocks.shape[0], blocks.shape[1]
    vectors, width = start_vectors.shape
    panel = width // size
    share = slots // n_col
    bf16, f32 = jnp.bfloat16, jnp.float32
    shape = jax.ShapeDtypeStruct

    rows, cols, ids = block_rows[0], block_cols[0], jnp.arange(slots, dtype=jnp.int32)
    owner = rows // panel
    earlier = (owner[None, :] == owner[:, None]) & (ids[None, :] < ids[:, None])
    place = owner * share + jnp.sum(earlier.astype(jnp.int32), axis=1)
    here = (place[None, :] == ids[:, None]).astype(jnp.int32)
    perm = jnp.sum(here * ids[None, :], axis=1)
    rows = jnp.sum(here * rows[None, :], axis=1)
    cols = jnp.sum(here * cols[None, :], axis=1)
    live = (perm < counts[0, 0]).astype(jnp.int32)

    row_ask = jnp.pad((rows % panel).reshape(n_col, 1, share), ((0, 0), (0, 0), (0, 128 - share)))
    col_ask = jnp.pad(cols.reshape(1, 1, slots), ((0, 0), (0, 0), (0, 128 - slots)))
    gram_shape = (8, vectors * vectors // 8)
    pieces = 4 if n_col % 4 == 0 else 1
    dma = pltpu.SemaphoreType.DMA
    order = float(n_row * n_col * width)
    mesh_sum = [
        pltpu.VMEM((n_row,) + gram_shape, f32),
        pltpu.VMEM(gram_shape, f32),
        pltpu.VMEM((n_col,) + gram_shape, f32),
        dma((n_row,)),
        dma((n_row,)),
        dma((n_col,)),
        dma((n_col,)),
    ]
    by_owner = (n_col, share, vectors, size)
    by_piece = (pieces, slots // pieces, vectors, size)
    product = gram = None
    for iteration in range(ITERS):
        first = iteration == 0
        if first:
            lists, sources = (row_ask, col_ask), (start_vectors,)
            list_shapes = (shape((n_col, 1, 128), jnp.int32), shape((n_row, 1, 128), jnp.int32))
        else:
            lists, sources, list_shapes = (wanted, all_cols), (product, gram), ()
        *got, row_terms, col_terms = pl.pallas_call(
            functools.partial(product_kernel, first, n_row, n_col, pieces, panel, order),
            out_shape=list_shapes + (shape(by_owner, bf16), shape((n_row,) + by_piece, bf16)),
            in_specs=([HBM] if first else [SMEM]) * 2
            + [SMEM] * 3
            + ([HBM] if first else [HBM, VMEM])
            + [HBM],
            out_specs=(HBM,) * (len(list_shapes) + 2),
            scratch_shapes=[
                pltpu.VMEM((panel, vectors, size), bf16),
                pltpu.VMEM(by_owner, bf16),
                pltpu.VMEM(by_owner, bf16),
                pltpu.VMEM(by_owner, bf16),
                pltpu.VMEM((n_row,) + by_piece, bf16),
                pltpu.VMEM((n_row,) + by_piece, bf16),
                pltpu.VMEM(by_piece, bf16),
                pltpu.VMEM(blocks.shape, bf16),
                dma((3 + pieces,)),
                dma((n_col,)),
                dma((n_col,)),
                dma((n_row, pieces)),
                dma((n_row, pieces)),
                dma((n_col,)),
                dma((n_col,)),
                dma((n_row, pieces)),
                dma((n_row, pieces)),
            ]
            + (
                [
                    pltpu.VMEM((vectors, width), f32),
                    pltpu.SMEM((n_col, 1, 128), jnp.int32),
                    pltpu.SMEM((n_row, 1, 128), jnp.int32),
                    dma((4,)),
                    dma((n_col,)),
                    dma((n_col,)),
                    dma((n_row,)),
                    dma((n_row,)),
                ]
                if first
                else [pltpu.VMEM((panel, vectors, size), f32)] + mesh_sum
            ),
            compiler_params=pltpu.CompilerParams(
                collective_id=1 if first else 2,
                has_side_effects=True,
                vmem_limit_bytes=VMEM_BYTES,
            ),
        )(*lists, perm, cols, live, *sources, blocks)
        if first:
            wanted, all_cols = got
        product, gram = pl.pallas_call(
            functools.partial(sum_kernel, n_col),
            out_shape=(shape((panel, vectors, size), f32), shape(gram_shape, f32)),
            in_specs=[SMEM, SMEM, HBM, HBM],
            out_specs=(VMEM, VMEM),
            scratch_shapes=[
                pltpu.VMEM((slots, vectors, size), bf16),
                pltpu.VMEM((n_row, slots, vectors, size), bf16),
                dma((2,)),
            ],
            compiler_params=local_params(),
        )(
            wanted,
            all_cols,
            row_terms.reshape(slots, vectors, size),
            col_terms.reshape(n_row, slots, vectors, size),
        )
    inverse = pl.pallas_call(
        functools.partial(factor_kernel, n_row, n_col, order),
        out_shape=shape((vectors, vectors), f32),
        in_specs=[VMEM],
        out_specs=VMEM,
        scratch_shapes=mesh_sum,
        compiler_params=pltpu.CompilerParams(
            collective_id=3, has_side_effects=True, vmem_limit_bytes=VMEM_BYTES
        ),
    )(gram)
    return pl.pallas_call(
        finish_kernel,
        out_shape=shape((vectors, width), f32),
        in_specs=[VMEM, VMEM],
        out_specs=VMEM,
        compiler_params=local_params(),
    )(product, inverse)


def solution(mesh):
    placed = (
        P("row", "col", None),
        P("row", "col"),
        P("row", "col"),
        P("row", "col"),
        P(None, ("row", "col")),
    )
    return jax.shard_map(
        functools.partial(per_device, mesh.shape["row"], mesh.shape["col"]),
        mesh=mesh,
        in_specs=placed,
        out_specs=P(None, ("row", "col")),
        check_vma=False,
    )
```
